32 devices in a mesh: space: 8 (over z, y), slab: 4 (over x, core).
Axes of the slice: x: 2, y: 2, z: 4, core: 2. Of those that a mesh axis runs over, the one named last changes fastest.
Arguments:
- features: float32 [128, 8, 8, 512], P(('space', 'slab')), may hold values from -6 to 6
- live: int32 [32], P(('space', 'slab')), may hold values from 1 to 4, as said below
- rim_slots: int32 [32, 2], P(('space', 'slab')), may hold values from 0 to 3, as said below
- neighbours: int32 [128, 26], P(('space', 'slab')), may hold values from 0 to 12, as said below
- weights: float32 [4, 27, 4096], replicated, may hold values from -0.15625 to 0.15625
- biases: float32 [4, 64], replicated, may hold values from -3 to 3
Outputs:
- output: float32 [128, 8, 8, 512], P(('space', 'slab'))
The draws below stay inside these ranges and needn't reach their ends.
Inputs may be any that keep to these rules, and one draw needn't show every extreme that they name: `live`: devices whose space indices differ by 8 / 2 (same slab index) hold at most 6 occupied bricks together; in every draw some pair holds exactly that and some device holds 4. `rim_slots`: every entry is below its device's live count. `neighbours`: entries below 4 are below the device's live count.
All inputs are finite; a program needn't handle non-finite values.
Results may differ from the reference program's by a relative error of at most 0.0003.
Values sent between devices are 32-bit elements; how exact they have to be, the bound alone decides.
A program may use at most 128 MiB of HBM per device.

```python
import jax
import jax.numpy as jnp
from jax import lax

CH = 64
CONVS = 4
B_DEV = 4
RIM = 2
LEND = 3
BRICKS = 128
N_SPACE = 8
N_SLAB = 4


def live_counts(key):
    base = jax.random.fold_in(key, 11)
    kone, ktwo, kthree, kfour = jax.random.split(base, 4)
    half = N_SPACE // 2
    pairs = half * N_SLAB
    heavy = jax.random.randint(kone, (pairs,), LEND, B_DEV + 1)
    spread = jax.random.randint(ktwo, (pairs,), 0, 1 << 20)
    light = 1 + spread % (2 * LEND - heavy)
    forced = jax.random.randint(kthree, (), 0, pairs)
    index = jnp.arange(pairs)
    heavy = jnp.where(index == forced, B_DEV, heavy)
    light = jnp.where(index == forced, 2 * LEND - B_DEV, light)
    flip = jax.random.randint(kfour, (pairs,), 0, 2)
    first = jnp.where(flip == 1, heavy, light).reshape(half, N_SLAB)
    second = jnp.where(flip == 1, light, heavy).reshape(half, N_SLAB)
    return jnp.concatenate([first, second], 0).reshape(-1).astype(jnp.int32)


def draw_live(key, part):
    return live_counts(key)


def draw_rim_slots(key, part):
    counts = live_counts(key)
    spread = jax.random.randint(jax.random.fold_in(key, 23), (N_SPACE * N_SLAB, RIM), 0, 1 << 20)
    return (spread % counts[:, None]).astype(jnp.int32)


def draw_neighbours(key, part):
    counts = live_counts(key)
    rows = N_SPACE * N_SLAB * B_DEV
    owner_live = jnp.repeat(counts, B_DEV)[:, None]
    kone, ktwo = jax.random.split(jax.random.fold_in(key, 37))
    kind = jax.random.randint(kone, (rows, 26), 0, 5)
    spread = jax.random.randint(ktwo, (rows, 26), 0, 1 << 20)
    own = spread % owner_live
    rim = B_DEV + spread % (4 * RIM)
    empty = jnp.full((rows, 26), B_DEV + 4 * RIM, jnp.int32)
    return jnp.where(kind < 2, own, jnp.where(kind < 4, rim, empty)).astype(jnp.int32)


def block_scale(stream_key, dims, cuts, smallest, top_value):
    level = 1.0
    for axis_at, blocks in cuts:
        heights = jax.random.uniform(jax.random.fold_in(jax.random.fold_in(stream_key, 6), axis_at), (blocks,), jnp.float32, smallest / len(cuts), top_value / len(cuts))
        level = level * jnp.repeat(jnp.exp(heights), dims[axis_at] // blocks).reshape((-1,) + (1,) * (len(dims) - 1 - axis_at))
    return level


def noise(stream_key, shape, deviation, most, cuts=(), held_as=jnp.bfloat16):
    factor_of = block_scale(stream_key, shape, cuts, -0.22, 0.18) if cuts else 1.0
    array = jax.random.normal(stream_key, shape, jnp.float32) * deviation * factor_of
    return jnp.minimum(jnp.maximum(array, -most), most).astype(held_as)


def setup_inputs(seed: int = 0) -> dict:
    arg_keys = jax.random.split(jax.random.key(seed), 7)
    return {
        "features": noise(arg_keys[0], (BRICKS, 8, 8, 8 * CH), 1.0, 6.0, ((0, 32),), jnp.float32),
        "live": draw_live(jax.random.fold_in(arg_keys[6], 71), 0),
        "rim_slots": draw_rim_slots(jax.random.fold_in(arg_keys[6], 71), 0),
        "neighbours": draw_neighbours(jax.random.fold_in(arg_keys[6], 71), 0),
        "weights": noise(arg_keys[4], (CONVS, 27, CH * CH), (27 * CH) ** -0.5, 0.15625, (), jnp.float32),
        "biases": noise(arg_keys[5], (CONVS, CH), 0.5, 3.0, (), jnp.float32),
    }


def direction_list():
    result = []
    for ddx in (-1, 0, 1):
        for ddy in (-1, 0, 1):
            for ddz in (-1, 0, 1):
                if (ddx, ddy, ddz) != (0, 0, 0):
                    result.append((ddx, ddy, ddz))
    return result


def source_index(step):
    if step == -1:
        return 7
    if step == 1:
        return 0
    return slice(0, 8)


def extent(step):
    return 8 if step == 0 else 1


def brick_piece(table, direction):
    ddx, ddy, ddz = direction
    channels = table.shape[-1] // 8
    cube = table.reshape(table.shape[0], 8, 8, 8, channels)
    return cube[:, source_index(ddx), source_index(ddy), source_index(ddz)]


def assemble(center, table, nbr, getter):
    count = center.shape[0]
    channels = center.shape[-1] // 8
    blocks = {(0, 0, 0): center.reshape(count, 8, 8, 8, channels)}
    for jdir, direction in enumerate(direction_list()):
        piece = getter(table, direction)[nbr[:, jdir]]
        blocks[direction] = piece.reshape(count, extent(direction[0]), extent(direction[1]), extent(direction[2]), channels)
    slabs = []
    for ddx in (-1, 0, 1):
        rows = []
        for ddy in (-1, 0, 1):
            rows.append(jnp.concatenate([blocks[(ddx, ddy, ddz)] for ddz in (-1, 0, 1)], 3))
        slabs.append(jnp.concatenate(rows, 2))
    return jnp.concatenate(slabs, 1)


def convolve(padded, kernel):
    count = padded.shape[0]
    channels = padded.shape[-1]
    taps = kernel.reshape(27, channels, channels)
    stacked = jnp.concatenate([padded[:, :, boff:boff + 8, coff:coff + 8, :] for boff in range(3) for coff in range(3)], -1)
    total = jnp.zeros((count * 512, channels), jnp.float32)
    for aoff in range(3):
        columns = stacked[:, aoff:aoff + 8].reshape(count * 512, 9 * channels)
        block = taps[aoff * 9:aoff * 9 + 9].reshape(9 * channels, channels)
        total = total + jnp.dot(columns, block, preferred_element_type=jnp.float32, precision=lax.Precision.HIGHEST)
    return total.reshape(count, 8, 8, 8 * channels)


def reference(features, live, rim_slots, neighbours, weights, biases):
    devices = N_SPACE * N_SLAB
    width = 8 * CH
    field = features.reshape(devices, B_DEV, 8, 8, width)
    mask = (jnp.arange(B_DEV, dtype=jnp.int32)[None, :] < live[:, None]).astype(jnp.float32)[:, :, None, None, None]
    nbr = neighbours.reshape(devices, B_DEV, 26)

    def layer(field, kidx):
        rims = jax.vmap(lambda rows, slots: rows[slots])(field, rim_slots)
        grid = rims.reshape(N_SPACE, N_SLAB, RIM, 8, 8, width)
        zero_row = jnp.zeros((1, N_SLAB, RIM, 8, 8, width), jnp.float32)
        zero_col = jnp.zeros((N_SPACE, 1, RIM, 8, 8, width), jnp.float32)
        low_space = jnp.concatenate([zero_row, grid[:-1]], 0)
        high_space = jnp.concatenate([grid[1:], zero_row], 0)
        low_slab = jnp.concatenate([zero_col, grid[:, :-1]], 1)
        high_slab = jnp.concatenate([grid[:, 1:], zero_col], 1)
        beside_all = jnp.concatenate([low_space, high_space, low_slab, high_slab], 2).reshape(devices, 4 * RIM, 8, 8, width)
        table = jnp.concatenate([field, beside_all, jnp.zeros((devices, 1, 8, 8, width), jnp.float32)], 1)

        def single(items):
            tab, cen, nb = items
            return convolve(assemble(cen, tab, nb, brick_piece), weights[kidx])

        return lax.map(single, (table, field, nbr))

    field = field * mask
    for blk in range(CONVS // 2):
        first = 2 * blk
        hidden = jax.nn.relu(layer(field, first) + jnp.tile(biases[first], 8)) * mask
        field = jax.nn.relu(field + layer(hidden, first + 1) + jnp.tile(biases[first + 1], 8)) * mask
    return field.reshape(devices * B_DEV, 8, 8, width)
```

```python
import functools

import jax
import jax.numpy as jnp
from jax import lax
from jax.experimental import pallas as pl
from jax.experimental.pallas import tpu as pltpu
from jax.sharding import PartitionSpec as P

MESH = pl.DeviceIdType.MESH
SIDE = 8


def direction_number(dx, dy, dz):
    index = 9 * (dx + 1) + 3 * (dy + 1) + (dz + 1)
    return index if index < 13 else index - 1


def layers_kernel(
    nsp, nsl, nbr, live, rim, feat, bias, w_hbm, out,
    cur, hid, own, offer, pad, cols, whi, wlo, wbuf, acc,
    wsem, ssem, rsem, *tabs,
):
    bricks = feat.shape[0]
    width = feat.shape[-1]
    ch = width // SIDE
    half = width // 2
    pair = 2 * ch
    ktile = half + pair
    kdy = 3 * ktile
    rims = offer.shape[1]
    convs = w_hbm.shape[0]
    sp = lax.axis_index("space")
    sl = lax.axis_index("slab")
    peers = (
        (sp > 0, (sp - 1, sl)),
        (sp < nsp - 1, (sp + 1, sl)),
        (sl > 0, (sp, sl - 1)),
        (sl < nsl - 1, (sp, sl + 1)),
    )

    barrier = pltpu.get_barrier_semaphore()
    for has, peer in peers:
        @pl.when(has)
        def _():
            pl.semaphore_signal(barrier, inc=1, device_id=peer, device_id_type=MESH)

    def weight_copy(k):
        return pltpu.make_async_copy(w_hbm.at[k], wbuf.at[k], wsem.at[k])

    for k in range(convs):
        weight_copy(k).start()

    def remote(k, d):
        first = bricks + rims * (d ^ 1)
        return pltpu.make_async_remote_copy(
            src_ref=offer.at[k],
            dst_ref=tabs[k].at[pl.ds(first, rims)],
            send_sem=ssem.at[k, d],
            recv_sem=rsem.at[k, d ^ 1],
            device_id=peers[d][1],
            device_id_type=MESH,
        )

    def mask_of(b):
        return jnp.where(b < live[0], 1.0, 0.0).astype(jnp.float32)

    low = lax.broadcasted_iota(jnp.int32, (SIDE, pair), 1) < ch
    low1 = lax.broadcasted_iota(jnp.int32, (1, pair), 1) < ch

    def take_faces(src, k):
        def one(b, carry):
            own[b, 0] = src[b, 0]
            own[b, 1] = src[b, SIDE - 1]
            for s, y in ((2, 0), (3, SIDE - 1)):
                for x in range(SIDE):
                    own[b, s, x:x + 1, :] = src[b, x, y:y + 1, :]
            for x in range(SIDE):
                at = (x % 4) * pair
                own[b, 4 + x // 4, :, at:at + pair] = jnp.where(
                    low, src[b, x, :, 0:pair], src[b, x, :, width - pair:width]
                )
            tabs[k][b] = own[b]
            return carry

        lax.fori_loop(0, bricks, one, 0)
        for r in range(rims):
            offer[k, r] = own[rim[0, r]]

    def send(k):
        for d in range(4):
            @pl.when(peers[d][0])
            def _():
                remote(k, d).start()

    def receive(k):
        for d in range(4):
            @pl.when(peers[d][0])
            def _():
                remote(k, d ^ 1).wait_recv()

    def finish_sends(k):
        for d in range(4):
            @pl.when(peers[d][0])
            def _():
                remote(k, d).wait_send()

    def build_weights(k):
        weight_copy(k).wait()

        def one(t, carry):
            a = t // 3
            base = pl.multiple_of((t - 3 * a) * ktile, ktile)
            for j in range(4):
                block = wbuf[k, t, j]
                hi = block.astype(jnp.bfloat16)
                lo = (block - hi.astype(jnp.float32)).astype(jnp.bfloat16)
                for q in range(2):
                    z = j - 1 + 2 * q
                    row = base + (z if z >= 0 else 5) * ch
                    row = pl.multiple_of(row, ch)
                    lanes = slice(q * pair, (q + 1) * pair)
                    whi[a, pl.ds(row, ch), lanes] = hi
                    whi[a, pl.ds(pl.multiple_of(row + kdy, ch), ch), lanes] = hi
                    wlo[a, pl.ds(row, ch), lanes] = lo
            return carry

        lax.fori_loop(0, 9, one, 0)

    def row_of(center, below, above, mask):
        return jnp.concatenate(
            [
                center[:, :half],
                jnp.where(mask, center[:, half:half + pair], below),
                center[:, half:],
                jnp.where(mask, above, center[:, half - pair:half]),
            ],
            axis=1,
        )

    def build_columns(src, k):
        tab = tabs[k]

        def one(b, carry):
            def entry(dx, dy, dz):
                return nbr[b, direction_number(dx, dy, dz)]

            for dx, xrow, s in ((-1, 0, 1), (1, SIDE + 1, 0)):
                pad[xrow, 1:SIDE + 1, :] = row_of(
                    tab[entry(dx, 0, 0), s],
                    tab[entry(dx, 0, -1), s, :, width - pair:width],
                    tab[entry(dx, 0, 1), s, :, 0:pair],
                    low,
                )
                for dy, yrow, y in ((-1, 0, SIDE - 1), (1, SIDE + 1, 0)):
                    pad[xrow, yrow:yrow + 1, :] = row_of(
                        tab[entry(dx, dy, 0), s, y:y + 1, :],
                        tab[entry(dx, dy, -1), s, y:y + 1, width - pair:width],
                        tab[entry(dx, dy, 1), s, y:y + 1, 0:pair],
                        low1,
                    )
            nlow, nhigh = entry(0, 0, -1), entry(0, 0, 1)
            for x in range(SIDE):
                at = (x % 4) * pair
                pad[1 + x, 1:SIDE + 1, :] = row_of(
                    src[b, x],
                    tab[nlow, 4 + x // 4, :, at:at + pair],
                    tab[nhigh, 4 + x // 4, :, at:at + pair],
                    low,
                )
            for dy, yrow, s in ((-1, 0, 3), (1, SIDE + 1, 2)):
                rows = row_of(
                    tab[entry(0, dy, 0), s],
                    tab[entry(0, dy, -1), s, :, width - pair:width],
                    tab[entry(0, dy, 1), s, :, 0:pair],
                    low,
                )
                for x in range(SIDE):
                    pad[1 + x, yrow:yrow + 1, :] = rows[x:x + 1]
            at = pl.multiple_of(b * 2 * SIDE, 2 * SIDE)
            for x in range(SIDE + 2):
                for dy in range(3):
                    v = pad[x, dy:dy + SIDE, :]
                    v = jnp.concatenate([v[:, :ktile], v[:, ktile:]], axis=0)
                    hi = v.astype(jnp.bfloat16)
                    lo = (v - hi.astype(jnp.float32)).astype(jnp.bfloat16)
                    cols[x, pl.ds(at, 2 * SIDE), dy * ktile:(dy + 1) * ktile] = hi
                    cols[x, pl.ds(at, 2 * SIDE), kdy + dy * ktile:kdy + (dy + 1) * ktile] = lo
            return carry

        lax.fori_loop(0, bricks, one, 0)

    def convolve():
        rows = SIDE * bricks * 2 * SIDE
        total = None
        for a in range(3):
            left = cols[a:a + SIDE].reshape(rows, 2 * kdy)
            term = jnp.dot(left, whi[a], preferred_element_type=jnp.float32)
            total = term if total is None else total + term
            left = cols[a:a + SIDE, :, :kdy].reshape(rows, kdy)
            total = total + jnp.dot(left, wlo[a], preferred_element_type=jnp.float32)
        acc[...] = total.reshape(acc.shape)

    def epilogue(k, res, dst):
        bvec = bias[k:k + 1, :]
        bvec = jnp.concatenate([bvec, bvec, bvec, bvec], axis=1)

        def one(b, carry):
            m = mask_of(b)
            for x in range(SIDE):
                for t in range(2):
                    at = pl.multiple_of(b * 2 * SIDE + t * SIDE, SIDE)
                    v = acc[x, pl.ds(at, SIDE), :] + bvec
                    lanes = slice(t * half, (t + 1) * half)
                    if res is not None:
                        v = v + res[b, x, :, lanes]
                    dst[b, x, :, lanes] = jnp.maximum(v, 0.0) * m
            return carry

        lax.fori_loop(0, bricks, one, 0)

    def mask_features(b, carry):
        cur[b] = feat[b] * mask_of(b)
        return carry

    lax.fori_loop(0, bricks, mask_features, 0)
    take_faces(cur, 0)
    arrivals = sum(jnp.where(has, 1, 0) for has, _ in peers)
    pl.semaphore_wait(barrier, arrivals)
    send(0)

    whi[...] = jnp.zeros_like(whi)
    wlo[...] = jnp.zeros_like(wlo)
    last = bricks + 4 * rims
    for k in range(convs):
        tabs[k][last] = jnp.zeros(tabs[k].shape[1:], jnp.float32)
    for d in range(4):
        @pl.when(jnp.logical_not(peers[d][0]))
        def _():
            for k in range(convs):
                for r in range(rims):
                    tabs[k][bricks + rims * d + r] = jnp.zeros(tabs[k].shape[1:], jnp.float32)

    for k in range(convs):
        src = cur if k % 2 == 0 else hid
        if k % 2 == 0:
            dst = hid
        else:
            dst = cur if k < convs - 1 else out
        build_weights(k)
        receive(k)
        build_columns(src, k)
        convolve()
        epilogue(k, None if k % 2 == 0 else cur, dst)
        if k < convs - 1:
            take_faces(dst, k + 1)
            send(k + 1)
    for k in range(convs):
        finish_sends(k)


def shards(nsp, nsl, features, live, rim_slots, neighbours, weights, biases):
    bricks, _, _, width = features.shape
    ch = biases.shape[-1]
    convs = weights.shape[0]
    rims = rim_slots.shape[-1]
    entries = bricks + 4 * rims + 1
    taps = weights.reshape(convs, 9, 3, ch, ch)
    none = jnp.zeros((convs, 9, 1, ch, ch), jnp.float32)
    blocks = jnp.concatenate(
        [jnp.concatenate([taps, none], 2), jnp.concatenate([none, taps], 2)], -1
    )
    half = width // 2
    kdy = 3 * (half + 2 * ch)
    f32, bf16 = jnp.float32, jnp.bfloat16
    smem = pl.BlockSpec(memory_space=pltpu.SMEM)
    vmem = pl.BlockSpec(memory_space=pltpu.VMEM)
    return pl.pallas_call(
        functools.partial(layers_kernel, nsp, nsl),
        out_shape=jax.ShapeDtypeStruct(features.shape, f32),
        in_specs=[smem, smem, smem, vmem, vmem, pl.BlockSpec(memory_space=pl.ANY)],
        out_specs=vmem,
        scratch_shapes=[
            pltpu.VMEM(features.shape, f32),
            pltpu.VMEM(features.shape, f32),
            pltpu.VMEM((bricks, 6, SIDE, width), f32),
            pltpu.VMEM((convs, rims, 6, SIDE, width), f32),
            pltpu.VMEM((SIDE + 2, 2 * SIDE, width + 4 * ch), f32),
            pltpu.VMEM((SIDE + 2, bricks * 2 * SIDE, 2 * kdy), bf16),
            pltpu.VMEM((3, 2 * kdy, half), bf16),
            pltpu.VMEM((3, kdy, half), bf16),
            pltpu.VMEM((convs, 9, 4, ch, 2 * ch), f32),
            pltpu.VMEM((SIDE, bricks * 2 * SIDE, half), f32),
            pltpu.SemaphoreType.DMA((convs,)),
            pltpu.SemaphoreType.DMA((convs, 4)),
            pltpu.SemaphoreType.DMA((convs, 4)),
        ]
        + [pltpu.VMEM((entries, 6, SIDE, width), f32) for _ in range(convs)],
        compiler_params=pltpu.CompilerParams(
            collective_id=0, has_side_effects=True, vmem_limit_bytes=56 * 1024 * 1024
        ),
        name="layers",
    )(neighbours, live, rim_slots, features, biases, blocks)


def solution(mesh):
    in_specs = (
        P(("space", "slab"), None, None, None),
        P(("space", "slab")),
        P(("space", "slab"), None),
        P(("space", "slab"), None),
        P(),
        P(),
    )
    out_specs = P(("space", "slab"), None, None, None)
    body = functools.partial(shards, mesh.shape["space"], mesh.shape["slab"])
    return jax.shard_map(body, mesh=mesh, in_specs=in_specs, out_specs=out_specs, check_vma=False)
```

```python
import functools

import jax
import jax.numpy as jnp
from jax import lax
from jax.experimental import pallas as pl
from jax.experimental.pallas import tpu as pltpu
from jax.sharding import PartitionSpec as P

MESH = pl.DeviceIdType.MESH
SIDE = 8


def direction_number(dx, dy, dz):
    index = 9 * (dx + 1) + 3 * (dy + 1) + (dz + 1)
    return index if index < 13 else index - 1


def layers_kernel(
    nsp, nsl, nbr, live, rim, feat, bias, w_hbm, out,
    cur, hid, own, offer, pad, cols, whi, wlo, wbuf, acc,
    wsem, ssem, rsem, *tabs,
):
    bricks = feat.shape[0]
    width = feat.shape[-1]
    ch = width // SIDE
    half = width // 2
    pair = 2 * ch
    ktile = half + pair
    kdy = 3 * ktile
    rims = offer.shape[1]
    convs = w_hbm.shape[1]
    sp = lax.axis_index("space")
    sl = lax.axis_index("slab")
    peers = (
        (sp > 0, (sp - 1, sl)),
        (sp < nsp - 1, (sp + 1, sl)),
        (sl > 0, (sp, sl - 1)),
        (sl < nsl - 1, (sp, sl + 1)),
    )

    barrier = pltpu.get_barrier_semaphore()
    for has, peer in peers:
        @pl.when(has)
        def _():
            pl.semaphore_signal(barrier, inc=1, device_id=peer, device_id_type=MESH)

    def weight_copy(k):
        return pltpu.make_async_copy(w_hbm.at[:, k], wbuf.at[k], wsem.at[k])

    for k in range(convs):
        weight_copy(k).start()

    def remote(k, d):
        first = bricks + rims * (d ^ 1)
        return pltpu.make_async_remote_copy(
            src_ref=offer.at[k],
            dst_ref=tabs[k].at[pl.ds(first, rims)],
            send_sem=ssem.at[k, d],
            recv_sem=rsem.at[k, d ^ 1],
            device_id=peers[d][1],
            device_id_type=MESH,
        )

    def mask_of(b):
        return jnp.where(b < live[0], 1.0, 0.0).astype(jnp.float32)

    low = lax.broadcasted_iota(jnp.int32, (SIDE, pair), 1) < ch
    low1 = lax.broadcasted_iota(jnp.int32, (1, pair), 1) < ch

    def take_faces(src, k):
        def one(b, carry):
            own[b, 0] = src[b, 0]
            own[b, 1] = src[b, SIDE - 1]
            for s, y in ((2, 0), (3, SIDE - 1)):
                for x in range(SIDE):
                    own[b, s, x:x + 1, :] = src[b, x, y:y + 1, :]
            for x in range(SIDE):
                at = (x % 4) * pair
                own[b, 4 + x // 4, :, at:at + pair] = jnp.where(
                    low, src[b, x, :, 0:pair], src[b, x, :, width - pair:width]
                )
            tabs[k][b] = own[b]
            return carry

        lax.fori_loop(0, bricks, one, 0)
        for r in range(rims):
            offer[k, r] = own[rim[0, r]]

    def send(k):
        for d in range(4):
            @pl.when(peers[d][0])
            def _():
                remote(k, d).start()

    def receive(k):
        for d in range(4):
            @pl.when(peers[d][0])
            def _():
                remote(k, d ^ 1).wait_recv()

    def finish_sends(k):
        for d in range(4):
            @pl.when(peers[d][0])
            def _():
                remote(k, d).wait_send()

    def build_weights(k):
        weight_copy(k).wait()

        def one(t, carry):
            a = t // 3
            base = pl.multiple_of((t - 3 * a) * ktile, ktile)
            taps = [wbuf[k, 3 * t + i] for i in range(3)]
            none = jnp.zeros((ch, ch), jnp.float32)
            for j in range(4):
                block = jnp.concatenate(
                    [taps[j] if j < 3 else none, taps[j - 1] if j > 0 else none], axis=1
                )
                hi = block.astype(jnp.bfloat16)
                lo = (block - hi.astype(jnp.float32)).astype(jnp.bfloat16)
                for q in range(2):
                    z = j - 1 + 2 * q
                    row = base + (z if z >= 0 else 5) * ch
                    row = pl.multiple_of(row, ch)
                    lanes = slice(q * pair, (q + 1) * pair)
                    whi[a, pl.ds(row, ch), lanes] = hi
                    whi[a, pl.ds(pl.multiple_of(row + kdy, ch), ch), lanes] = hi
                    wlo[a, pl.ds(row, ch), lanes] = lo
            return carry

        lax.fori_loop(0, 9, one, 0)

    def row_of(center, below, above, mask):
        return jnp.concatenate(
            [
                center[:, :half],
                jnp.where(mask, center[:, half:half + pair], below),
                center[:, half:],
                jnp.where(mask, above, center[:, half - pair:half]),
            ],
            axis=1,
        )

    def build_columns(src, k):
        tab = tabs[k]

        def one(b, carry):
            def entry(dx, dy, dz):
                return nbr[b, direction_number(dx, dy, dz)]

            for dx, xrow, s in ((-1, 0, 1), (1, SIDE + 1, 0)):
                pad[xrow, 1:SIDE + 1, :] = row_of(
                    tab[entry(dx, 0, 0), s],
                    tab[entry(dx, 0, -1), s, :, width - pair:width],
                    tab[entry(dx, 0, 1), s, :, 0:pair],
                    low,
                )
                for dy, yrow, y in ((-1, 0, SIDE - 1), (1, SIDE + 1, 0)):
                    pad[xrow, yrow:yrow + 1, :] = row_of(
                        tab[entry(dx, dy, 0), s, y:y + 1, :],
                        tab[entry(dx, dy, -1), s, y:y + 1, width - pair:width],
                        tab[entry(dx, dy, 1), s, y:y + 1, 0:pair],
                        low1,
                    )
            nlow, nhigh = entry(0, 0, -1), entry(0, 0, 1)
            for x in range(SIDE):
                at = (x % 4) * pair
                pad[1 + x, 1:SIDE + 1, :] = row_of(
                    src[b, x],
                    tab[nlow, 4 + x // 4, :, at:at + pair],
                    tab[nhigh, 4 + x // 4, :, at:at + pair],
                    low,
                )
            for dy, yrow, s in ((-1, 0, 3), (1, SIDE + 1, 2)):
                rows = row_of(
                    tab[entry(0, dy, 0), s],
                    tab[entry(0, dy, -1), s, :, width - pair:width],
                    tab[entry(0, dy, 1), s, :, 0:pair],
                    low,
                )
                for x in range(SIDE):
                    pad[1 + x, yrow:yrow + 1, :] = rows[x:x + 1]
            at = pl.multiple_of(b * 2 * SIDE, 2 * SIDE)
            for x in range(SIDE + 2):
                for dy in range(3):
                    v = pad[x, dy:dy + SIDE, :]
                    v = jnp.concatenate([v[:, :ktile], v[:, ktile:]], axis=0)
                    hi = v.astype(jnp.bfloat16)
                    lo = (v - hi.astype(jnp.float32)).astype(jnp.bfloat16)
                    cols[x, pl.ds(at, 2 * SIDE), dy * ktile:(dy + 1) * ktile] = hi
                    cols[x, pl.ds(at, 2 * SIDE), kdy + dy * ktile:kdy + (dy + 1) * ktile] = lo
            return carry

        lax.fori_loop(0, bricks, one, 0)

    def convolve():
        rows = SIDE * bricks * 2 * SIDE
        total = None
        for a in range(3):
            left = cols[a:a + SIDE].reshape(rows, 2 * kdy)
            term = jnp.dot(left, whi[a], preferred_element_type=jnp.float32)
            total = term if total is None else total + term
            left = cols[a:a + SIDE, :, :kdy].reshape(rows, kdy)
            total = total + jnp.dot(left, wlo[a], preferred_element_type=jnp.float32)
        acc[...] = total.reshape(acc.shape)

    def epilogue(k, res, dst):
        bvec = bias[k:k + 1, :]
        bvec = jnp.concatenate([bvec, bvec, bvec, bvec], axis=1)

        def one(b, carry):
            m = mask_of(b)
            for x in range(SIDE):
                for t in range(2):
                    at = pl.multiple_of(b * 2 * SIDE + t * SIDE, SIDE)
                    v = acc[x, pl.ds(at, SIDE), :] + bvec
                    lanes = slice(t * half, (t + 1) * half)
                    if res is not None:
                        v = v + res[b, x, :, lanes]
                    dst[b, x, :, lanes] = jnp.maximum(v, 0.0) * m
            return carry

        lax.fori_loop(0, bricks, one, 0)

    def mask_features(b, carry):
        cur[b] = feat[b] * mask_of(b)
        return carry

    lax.fori_loop(0, bricks, mask_features, 0)
    take_faces(cur, 0)
    arrivals = sum(jnp.where(has, 1, 0) for has, _ in peers)
    pl.semaphore_wait(barrier, arrivals)
    send(0)

    whi[...] = jnp.zeros_like(whi)
    wlo[...] = jnp.zeros_like(wlo)
    last = bricks + 4 * rims
    for k in range(convs):
        tabs[k][last] = jnp.zeros(tabs[k].shape[1:], jnp.float32)
    for d in range(4):
        @pl.when(jnp.logical_not(peers[d][0]))
        def _():
            for k in range(convs):
                for r in range(rims):
                    tabs[k][bricks + rims * d + r] = jnp.zeros(tabs[k].shape[1:], jnp.float32)

    for k in range(convs):
        src = cur if k % 2 == 0 else hid
        if k % 2 == 0:
            dst = hid
        else:
            dst = cur if k < convs - 1 else out
        build_weights(k)
        receive(k)
        build_columns(src, k)
        convolve()
        epilogue(k, None if k % 2 == 0 else cur, dst)
        if k < convs - 1:
            take_faces(dst, k + 1)
            send(k + 1)
    for k in range(convs):
        finish_sends(k)


def shards(nsp, nsl, features, live, rim_slots, neighbours, weights, biases):
    bricks, _, _, width = features.shape
    ch = biases.shape[-1]
    convs = weights.shape[0]
    rims = rim_slots.shape[-1]
    entries = bricks + 4 * rims + 1
    taps = weights.transpose(1, 0, 2).reshape(weights.shape[1], convs, ch, ch)
    half = width // 2
    kdy = 3 * (half + 2 * ch)
    f32, bf16 = jnp.float32, jnp.bfloat16
    smem = pl.BlockSpec(memory_space=pltpu.SMEM)
    vmem = pl.BlockSpec(memory_space=pltpu.VMEM)
    return pl.pallas_call(
        functools.partial(layers_kernel, nsp, nsl),
        out_shape=jax.ShapeDtypeStruct(features.shape, f32),
        in_specs=[smem, smem, smem, vmem, vmem, pl.BlockSpec(memory_space=pl.ANY)],
        out_specs=vmem,
        scratch_shapes=[
            pltpu.VMEM(features.shape, f32),
            pltpu.VMEM(features.shape, f32),
            pltpu.VMEM((bricks, 6, SIDE, width), f32),
            pltpu.VMEM((convs, rims, 6, SIDE, width), f32),
            pltpu.VMEM((SIDE + 2, 2 * SIDE, width + 4 * ch), f32),
            pltpu.VMEM((SIDE + 2, bricks * 2 * SIDE, 2 * kdy), bf16),
            pltpu.VMEM((3, 2 * kdy, half), bf16),
            pltpu.VMEM((3, kdy, half), bf16),
            pltpu.VMEM((convs, weights.shape[1], ch, ch), f32),
            pltpu.VMEM((SIDE, bricks * 2 * SIDE, half), f32),
            pltpu.SemaphoreType.DMA((convs,)),
            pltpu.SemaphoreType.DMA((convs, 4)),
            pltpu.SemaphoreType.DMA((convs, 4)),
        ]
        + [pltpu.VMEM((entries, 6, SIDE, width), f32) for _ in range(convs)],
        compiler_params=pltpu.CompilerParams(
            collective_id=0, has_side_effects=True, vmem_limit_bytes=56 * 1024 * 1024
        ),
        name="layers",
    )(neighbours, live, rim_slots, features, biases, taps)


def solution(mesh):
    in_specs = (
        P(("space", "slab"), None, None, None),
        P(("space", "slab")),
        P(("space", "slab"), None),
        P(("space", "slab"), None),
        P(),
        P(),
    )
    out_specs = P(("space", "slab"), None, None, None)
    body = functools.partial(shards, mesh.shape["space"], mesh.shape["slab"])
    return jax.shard_map(body, mesh=mesh, in_specs=in_specs, out_specs=out_specs, check_vma=False)
```
